32 devices in a mesh: dp: 2 (over core), mrow: 8 (over z, y), mcol: 2 (over x).
Axes of the slice: x: 2, y: 2, z: 4, core: 2. Of those that a mesh axis runs over, the one named last changes fastest.
Arguments:
- grad_parts: bfloat16 [2, 18432, 8192], P('dp', 'mrow', 'mcol'), may hold values from -24 to 24, as said below
- master: float32 [18432, 8192], P('mrow', ('mcol', 'dp')), may hold values from -6 to 6
- row_factor: float32 [18432], P('mrow'), may hold values from 0.5 to 5
- col_factor: float32 [8192], P(('mcol', 'dp')), may hold values from 0.5 to 5
Outputs:
- new_master: float32 [18432, 8192], P('mrow', ('mcol', 'dp'))
- new_weights: bfloat16 [18432, 8192], P('mrow', 'mcol')
- new_rows: float32 [18432], P('mrow')
- new_cols: float32 [8192], P(('mcol', 'dp'))
- step: float32 [18432, 8192], P('mrow', ('mcol', 'dp'))
- root_mean: float32 [], replicated
The draws below stay inside these ranges and needn't reach their ends.
Inputs may be any that keep to these rules, and one draw needn't show every extreme that they name: `grad_parts`: each slice along the first dimension is one data-parallel group's partial gradient.
All inputs are finite; a program needn't handle non-finite values.
Results may differ from the reference program's by a relative error of at most 0.009.
Values may be sent and summed in bfloat16 or wider, within the bound.
A program may use at most 192 MiB of HBM per device.

```python
import math
import jax
import jax.numpy as jnp
from jax import lax

D = 8192
FF = 18432
N_DP = 2
N_MCOL = 2


def draw_grad_parts(key, part):
    key_rows = jax.random.fold_in(jax.random.fold_in(key, 17), 0)
    key_cols = jax.random.fold_in(jax.random.fold_in(key, 17), 1)
    key_own = jax.random.fold_in(jax.random.fold_in(key, 17), 3)
    row_scale = jnp.exp(0.5 * jnp.log(10.0) * jax.random.uniform(key_rows, (FF,), jnp.float32))
    col_scale = jnp.exp(0.5 * jnp.log(10.0) * jax.random.uniform(key_cols, (D,), jnp.float32))
    group_width = D // N_MCOL
    position = jnp.arange(D, dtype=jnp.float32) % group_width / (group_width - 1)
    rising = jnp.exp(0.5 * jnp.log(10.0) * position)
    base = 0.5 * jax.random.truncated_normal(key_own, -4.0, 4.0, (N_DP, FF, D), jnp.float32)
    col_all = 0.35 * col_scale * rising
    return (base * row_scale[None, :, None] * col_all[None, None, :]).astype(jnp.bfloat16)


def shard_levels(rng, shape, cuts, least, largest):
    loudness, own = 1.0, jax.random.fold_in(rng, 6)
    for dim, shards_of in cuts:
        steps = jnp.exp(jax.random.uniform(jax.random.fold_in(own, dim), (shards_of,), jnp.float32, least / len(cuts), largest / len(cuts)))
        loudness = loudness * jnp.repeat(steps, shape[dim] // shards_of).reshape([-1 if axis == dim else 1 for axis in range(len(shape))])
    return loudness


def gaussian(key, dims, width, limit, pieces=(), kind=jnp.bfloat16):
    gain = shard_levels(key, dims, pieces, -0.22, 0.18) if pieces else 1.0
    values = jax.random.normal(key, dims, jnp.float32) * width * gain
    return jnp.minimum(jnp.maximum(values, -limit), limit).astype(kind)


def setup_inputs(seed: int = 0) -> dict:
    arg_keys = jax.random.split(jax.random.key(seed), 5)
    grad_parts = draw_grad_parts(jax.random.fold_in(arg_keys[4], 71), 0)
    master = gaussian(arg_keys[1], (FF, D), 1.0, 6.0, ((0, 8), (1, 4)), jnp.float32)
    row_factor = jnp.clip(jnp.exp(math.log(5.0) - 2.3025851 * jax.random.uniform(arg_keys[2], (FF,), jnp.float32) ** shard_levels(arg_keys[2], (FF,), ((0, 8),), -0.2, 0.2)), 0.5, 5.0)
    col_factor = jnp.clip(jnp.exp(math.log(5.0) - 2.3025851 * jax.random.uniform(arg_keys[3], (D,), jnp.float32) ** shard_levels(arg_keys[3], (D,), ((0, 4),), -0.2, 0.2)), 0.5, 5.0)
    return {"grad_parts": grad_parts, "master": master, "row_factor": row_factor, "col_factor": col_factor}


DECAY_RATE = 1.0 - 10.0 ** (-0.8)
LEARN_RATE = 0.01
CLIP_LIMIT = 1.0
SQUARE_FLOOR = 1e-30

def reference(grad_parts, master, row_factor, col_factor):
    grad = jnp.zeros((FF, D), jnp.float32)
    for index in range(N_DP):
        grad = grad + grad_parts[index].astype(jnp.float32)
    squares = grad * grad + SQUARE_FLOOR
    new_rows = DECAY_RATE * row_factor + (1.0 - DECAY_RATE) * lax.optimization_barrier(jnp.sum(squares, axis=1)) / D
    new_cols = DECAY_RATE * col_factor + (1.0 - DECAY_RATE) * lax.optimization_barrier(jnp.sum(squares, axis=0)) / FF
    total = jnp.sum(new_rows) / FF
    second = new_rows[:, None] * new_cols[None, :] / total
    update = grad / jnp.sqrt(second)
    root_mean = jnp.sqrt(jnp.sum(update * update) / (FF * D))
    step = update / jnp.maximum(1.0, root_mean / CLIP_LIMIT)
    new_master = master - LEARN_RATE * step
    return (new_master, new_master.astype(jnp.bfloat16), new_rows, new_cols, step, root_mean)
```

```python
import functools

import jax
import jax.numpy as jnp
from jax import lax
from jax.experimental import pallas as pl
from jax.experimental.pallas import tpu as pltpu
from jax.sharding import PartitionSpec as P

DECAY_RATE = 1.0 - 10.0 ** (-0.8)
LEARN_RATE = 0.01
CLIP_LIMIT = 1.0
SQUARE_FLOOR = 1e-30
MESH = pl.DeviceIdType.MESH
LANES = 128
GROUP = 16


def chunk_of(rows, most=256):
    for size in range(min(most, rows), 0, -GROUP):
        if size % GROUP == 0 and rows % size == 0:
            return size
    return rows


def stats_kernel(
    n_dp, n_mrow, n_mcol, chunk,
    grad_ref, master_ref, old_rows_ref, old_cols_ref,
    g_ref, w_recv_ref, new_rows_ref, new_cols_ref, scal_ref,
    gbuf, recv, mbuf, row_col, row_slots, col_slots, sc1_slots, sc2_slots, inv_rows, col_acc,
    own_sem, gsend, grecv, rsend, rrecv, csend, crecv, s1send, s1recv, s2send, s2recv,
    wsend, wrecv, msem, osem,
):
    rows, wc = mbuf.shape
    nc = rows // chunk
    blocks = wc // LANES
    steps = chunk // GROUP
    n_row = n_dp * n_mcol
    width = wc * n_row
    height = rows * n_mrow
    dp, mrow, mcol = lax.axis_index("dp"), lax.axis_index("mrow"), lax.axis_index("mcol")
    q = dp * n_mcol + mcol

    def dp_peer(k):
        return {"dp": lax.rem(dp + k, n_dp), "mrow": mrow, "mcol": mcol}

    def row_peer(k):
        other = lax.rem(q + k, n_row)
        return {"dp": other // n_mcol, "mrow": mrow, "mcol": lax.rem(other, n_mcol)}

    def col_peer(k):
        return {"dp": dp, "mrow": lax.rem(mrow + k, n_mrow), "mcol": mcol}

    def loop(lo, hi, body):
        lax.fori_loop(lo, hi, lambda i, c: (body(i), c)[1], 0)

    def part(i):
        return pl.ds(pl.multiple_of(i * chunk, chunk), chunk)

    def own_copy(i):
        cols = pl.ds(pl.multiple_of(dp * wc, LANES), wc)
        return pltpu.make_async_copy(grad_ref.at[0, part(i), cols], gbuf.at[part(i)], own_sem.at[i])

    def grad_copy(k, i):
        cols = pl.ds(pl.multiple_of(lax.rem(dp + k, n_dp) * wc, LANES), wc)
        return pltpu.make_async_remote_copy(
            src_ref=grad_ref.at[0, part(i), cols], dst_ref=recv.at[k - 1, part(i)],
            send_sem=gsend.at[k - 1, i], recv_sem=grecv.at[k - 1, i],
            device_id=dp_peer(k), device_id_type=MESH)

    def master_copy(i):
        return pltpu.make_async_copy(master_ref.at[part(i)], mbuf.at[part(i)], msem.at[i])

    def out_copy(i):
        return pltpu.make_async_copy(gbuf.at[part(i)], g_ref.at[part(i)], osem.at[i])

    def weight_copy(k, i):
        return pltpu.make_async_remote_copy(
            src_ref=recv.at[0, part(i)], dst_ref=w_recv_ref.at[n_dp - 1 - k, part(i)],
            send_sem=wsend.at[k - 1, i], recv_sem=wrecv.at[k - 1, i],
            device_id=dp_peer(k), device_id_type=MESH)

    def slot_copy(slots, index, peer, send, recv_, k):
        return pltpu.make_async_remote_copy(
            src_ref=slots.at[index], dst_ref=slots.at[index],
            send_sem=send.at[k], recv_sem=recv_.at[k],
            device_id=peer(k), device_id_type=MESH)

    def send_slots(slots, index, peer, send, recv_, n):
        loop(1, n, lambda k: slot_copy(slots, index, peer, send, recv_, k).start())

    def wait_slots(slots, index, peer, send, recv_, n):
        loop(1, n, lambda k: slot_copy(slots, index, peer, send, recv_, k).wait())

    loop(0, nc, lambda i: own_copy(i).start())

    barrier = pltpu.get_barrier_semaphore()
    loop(1, n_row, lambda k: pl.semaphore_signal(barrier, inc=1, device_id=row_peer(k), device_id_type=MESH))
    loop(1, n_mrow, lambda k: pl.semaphore_signal(barrier, inc=1, device_id=col_peer(k), device_id_type=MESH))
    pl.semaphore_wait(barrier, n_row + n_mrow - 2)

    loop(0, nc, lambda i: [grad_copy(k, i).start() for k in range(1, n_dp)])
    loop(0, nc, lambda i: master_copy(i).start())

    col_acc[...] = jnp.zeros_like(col_acc)

    def sum_chunk(i):
        own_copy(i).wait()
        for k in range(1, n_dp):
            grad_copy(k, i).wait_recv()
        base = i * chunk

        def sum_rows(s, carry):
            at = pl.ds(pl.multiple_of(base + s * GROUP, GROUP), GROUP)
            row = None
            for b in range(blocks):
                lanes = slice(b * LANES, (b + 1) * LANES)
                g = gbuf[at, lanes].astype(jnp.float32)
                for k in range(n_dp - 1):
                    g = g + recv[k, at, lanes].astype(jnp.float32)
                gbuf[at, lanes] = g.astype(jnp.bfloat16)
                square = g * g + SQUARE_FLOOR
                row = square if row is None else row + square
                col_acc[:, lanes] += square[:8] + square[8:]
            row_col[pl.ds(pl.multiple_of(base + s * GROUP, GROUP), GROUP), :] = row
            return carry

        lax.fori_loop(0, steps, sum_rows, 0)
        out_copy(i).start()
        row_slots[q, :, part(i)] = jnp.sum(row_col[part(i), :].T, axis=0, keepdims=True)

    loop(0, nc, sum_chunk)
    col_slots[mrow] = jnp.sum(col_acc[...], axis=0, keepdims=True)
    send_slots(col_slots, mrow, col_peer, csend, crecv, n_mrow)
    send_slots(row_slots, q, row_peer, rsend, rrecv, n_row)
    wait_slots(row_slots, q, row_peer, rsend, rrecv, n_row)
    row_sum = row_slots[0]
    for j in range(1, n_row):
        row_sum = row_sum + row_slots[j]
    new_rows = DECAY_RATE * old_rows_ref[...] + (1.0 - DECAY_RATE) * row_sum / width
    new_rows_ref[...] = new_rows
    inv_rows[...] = lax.rsqrt(new_rows)
    row_mass = jnp.sum(new_rows)

    def spread(i):
        row_col[part(i), :] = jnp.broadcast_to(inv_rows[:, part(i)], (LANES, chunk)).T

    loop(0, nc, spread)
    wait_slots(col_slots, mrow, col_peer, csend, crecv, n_mrow)
    col_sum = lax.fori_loop(1, n_mrow, lambda j, acc: acc + col_slots[j], col_slots[0])
    new_cols = DECAY_RATE * old_cols_ref[...] + (1.0 - DECAY_RATE) * col_sum / height
    new_cols_ref[...] = new_cols
    inv_cols = 1.0 / new_cols
    col_acc[...] = jnp.broadcast_to(inv_cols, col_acc.shape)

    def square_rows(s, acc):
        at = pl.ds(pl.multiple_of(s * GROUP, GROUP), GROUP)
        row = None
        for b in range(blocks):
            lanes = slice(b * LANES, (b + 1) * LANES)
            g = gbuf[at, lanes].astype(jnp.float32)
            c = col_acc[:, lanes]
            term = g * g * jnp.concatenate([c, c], axis=0)
            row = term if row is None else row + term
        r = row_col[at, :]
        return acc + row * (r * r)

    acc = lax.fori_loop(0, rows // GROUP, square_rows, jnp.zeros((GROUP, LANES), jnp.float32))
    lane = lax.broadcasted_iota(jnp.int32, (1, LANES), 1)
    sc1_slots[mrow] = jnp.where(lane == 0, row_mass, jnp.where(lane == 1, jnp.sum(acc), 0.0))
    send_slots(sc1_slots, mrow, col_peer, s1send, s1recv, n_mrow)
    wait_slots(sc1_slots, mrow, col_peer, s1send, s1recv, n_mrow)
    sc2_slots[q] = lax.fori_loop(1, n_mrow, lambda j, a: a + sc1_slots[j], sc1_slots[0])
    send_slots(sc2_slots, q, row_peer, s2send, s2recv, n_row)
    wait_slots(sc2_slots, q, row_peer, s2send, s2recv, n_row)
    both = sc2_slots[0]
    for j in range(1, n_row):
        both = both + sc2_slots[j]
    pick = jnp.zeros((8, LANES), jnp.float32)
    total = jnp.sum(jnp.where(lane == 0, both, 0.0), axis=1, keepdims=True) / (n_row * height)
    whole = jnp.sum(jnp.where(lane == 1, both, 0.0), axis=1, keepdims=True)
    root_mean = jnp.sqrt(total * whole / (float(width) * float(height)))
    scale = jnp.sqrt(total) / jnp.maximum(1.0, root_mean / CLIP_LIMIT)
    scal_ref[0:1, :] = jnp.broadcast_to(root_mean, (1, LANES))
    scal_ref[1:2, :] = jnp.broadcast_to(scale, (1, LANES))
    col_acc[...] = jnp.broadcast_to(lax.rsqrt(new_cols) * scale, col_acc.shape)

    def weight_chunk(i):
        master_copy(i).wait()

        for k in range(1, n_dp):
            grad_copy(k, i).wait_send()

        def weight_rows(s, carry):
            at = pl.ds(pl.multiple_of(i * chunk + s * GROUP, GROUP), GROUP)
            r = row_col[at, :]
            for b in range(blocks):
                lanes = slice(b * LANES, (b + 1) * LANES)
                c = col_acc[:, lanes]
                step = gbuf[at, lanes].astype(jnp.float32) * r * jnp.concatenate([c, c], axis=0)
                recv[0, at, lanes] = (mbuf[at, lanes] - LEARN_RATE * step).astype(jnp.bfloat16)
            return carry

        lax.fori_loop(0, steps, weight_rows, 0)
        for k in range(1, n_dp):
            weight_copy(k, i).start()

    loop(0, nc, weight_chunk)

    def finish(i):
        out_copy(i).wait()
        for k in range(1, n_dp):
            weight_copy(k, i).wait()

    loop(0, nc, finish)


def final_kernel(
    n_dp, scal_ref, rows_ref, cols_ref, g_ref, master_ref, w_recv_ref,
    new_ref, weights_ref, step_ref, row_col, col_acc,
):
    chunk, wc = g_ref.shape
    dp = lax.axis_index("dp")

    @pl.when(pl.program_id(0) == 0)
    def _():
        scale = scal_ref[1:2, 0:1]
        col_acc[...] = jnp.broadcast_to(lax.rsqrt(cols_ref[...]) * scale, col_acc.shape)

    row_col[...] = jnp.broadcast_to(lax.rsqrt(rows_ref[0]), (LANES, chunk)).T

    def rows_of(start):
        def body(s, carry):
            at = pl.ds(pl.multiple_of(s * GROUP, GROUP), GROUP)
            r = row_col[at, :]
            for b in range(wc // LANES):
                lanes = slice(b * LANES, (b + 1) * LANES)
                c = col_acc[:, lanes]
                step = g_ref[at, lanes].astype(jnp.float32) * r * jnp.concatenate([c, c], axis=0)
                new = master_ref[at, lanes] - LEARN_RATE * step
                step_ref[at, lanes] = step
                new_ref[at, lanes] = new
                weights_ref[at, start + b * LANES:start + (b + 1) * LANES] = new.astype(jnp.bfloat16)
            return carry

        lax.fori_loop(0, chunk // GROUP, body, 0)

    for p in range(n_dp):
        @pl.when(dp == p)
        def _():
            rows_of(p * wc)
            for k in range(1, n_dp):
                start = (p + k) % n_dp * wc
                weights_ref[:, start:start + wc] = w_recv_ref[k - 1]


def on_device(n_dp, n_mrow, n_mcol, grad_parts, master, row_factor, col_factor):
    rows, wc = master.shape
    chunk = chunk_of(rows)
    nc = rows // chunk
    n_row = n_dp * n_mcol
    f32, bf16 = jnp.float32, jnp.bfloat16
    dma = pltpu.SemaphoreType.DMA
    anywhere = pl.BlockSpec(memory_space=pl.ANY)
    vmem = pl.BlockSpec(memory_space=pltpu.VMEM)
    peers = max(n_dp - 1, 1)
    g, w_recv, new_rows, new_cols, scal = pl.pallas_call(
        functools.partial(stats_kernel, n_dp, n_mrow, n_mcol, chunk),
        out_shape=(
            jax.ShapeDtypeStruct((rows, wc), bf16),
            jax.ShapeDtypeStruct((peers, rows, wc), bf16),
            jax.ShapeDtypeStruct((1, rows), f32),
            jax.ShapeDtypeStruct((1, wc), f32),
            jax.ShapeDtypeStruct((8, LANES), f32),
        ),
        in_specs=[anywhere, anywhere, vmem, vmem],
        out_specs=(anywhere, anywhere, vmem, vmem, vmem),
        scratch_shapes=[
            pltpu.VMEM((rows, wc), bf16),
            pltpu.VMEM((peers, rows, wc), bf16),
            pltpu.VMEM((rows, wc), f32),
            pltpu.VMEM((rows, LANES), f32),
            pltpu.VMEM((n_row, 1, rows), f32),
            pltpu.VMEM((n_mrow, 1, wc), f32),
            pltpu.VMEM((n_mrow, 1, LANES), f32),
            pltpu.VMEM((n_row, 1, LANES), f32),
            pltpu.VMEM((1, rows), f32),
            pltpu.VMEM((8, wc), f32),
            dma((nc,)), dma((peers, nc)), dma((peers, nc)),
            dma((n_row,)), dma((n_row,)), dma((n_mrow,)), dma((n_mrow,)),
            dma((n_mrow,)), dma((n_mrow,)), dma((n_row,)), dma((n_row,)),
            dma((peers, nc)), dma((peers, nc)), dma((nc,)), dma((nc,)),
        ],
        compiler_params=pltpu.CompilerParams(
            collective_id=0, has_side_effects=True, vmem_limit_bytes=56 * 2**20
        ),
        name="stats",
    )(grad_parts, master, row_factor.reshape(1, rows), col_factor.reshape(1, wc))

    tile = pl.BlockSpec((chunk, wc), lambda i: (i, 0))
    new_master, weights, step = pl.pallas_call(
        functools.partial(final_kernel, n_dp),
        grid=(nc,),
        out_shape=(
            jax.ShapeDtypeStruct((rows, wc), f32),
            jax.ShapeDtypeStruct((rows, n_dp * wc), bf16),
            jax.ShapeDtypeStruct((rows, wc), f32),
        ),
        in_specs=[
            pl.BlockSpec((8, LANES), lambda i: (0, 0)),
            pl.BlockSpec((1, 1, chunk), lambda i: (i, 0, 0)),
            pl.BlockSpec((1, wc), lambda i: (0, 0)),
            tile,
            tile,
            pl.BlockSpec((peers, chunk, wc), lambda i: (0, i, 0)),
        ],
        out_specs=(tile, pl.BlockSpec((chunk, n_dp * wc), lambda i: (i, 0)), tile),
        scratch_shapes=[pltpu.VMEM((chunk, LANES), f32), pltpu.VMEM((8, wc), f32)],
        compiler_params=pltpu.CompilerParams(vmem_limit_bytes=56 * 2**20),
        name="final",
    )(scal, new_rows.reshape(nc, 1, chunk), new_cols, g, master, w_recv)
    return (
        new_master,
        weights,
        new_rows.reshape(rows),
        new_cols.reshape(wc),
        step,
        scal[0, 0],
    )


def solution(mesh):
    placed = (P("dp", "mrow", "mcol"), P("mrow", ("mcol", "dp")), P("mrow"), P(("mcol", "dp")))
    sizes = (mesh.shape["dp"], mesh.shape["mrow"], mesh.shape["mcol"])
    return jax.shard_map(
        functools.partial(on_device, *sizes),
        mesh=mesh,
        in_specs=placed,
        out_specs=(
            P("mrow", ("mcol", "dp")),
            P("mrow", "mcol"),
            P("mrow"),
            P(("mcol", "dp")),
            P("mrow", ("mcol", "dp")),
            P(),
        ),
        check_vma=False,
    )
```

```python
import functools

import jax
import jax.numpy as jnp
from jax import lax
from jax.experimental import pallas as pl
from jax.experimental.pallas import tpu as pltpu
from jax.sharding import PartitionSpec as P

DECAY_RATE = 1.0 - 10.0 ** (-0.8)
LEARN_RATE = 0.01
CLIP_LIMIT = 1.0
SQUARE_FLOOR = 1e-30
MESH = pl.DeviceIdType.MESH
LANES = 128
GROUP = 16


def chunk_of(rows, most=256):
    for size in range(min(most, rows), 0, -GROUP):
        if size % GROUP == 0 and rows % size == 0:
            return size
    return rows


def stats_kernel(
    n_dp, n_mrow, n_mcol, chunk,
    grad_ref, master_ref, old_rows_ref, old_cols_ref,
    gbuf, recv, w_recv_ref, mbuf, row_col, new_rows_ref, new_cols_ref, scal_ref,
    row_slots, col_slots, sc1_slots, sc2_slots, inv_rows, col_acc,
    own_sem, gsend, grecv, rsend, rrecv, csend, crecv, s1send, s1recv, s2send, s2recv,
    wsend, wrecv, msem,
):
    rows, wc = mbuf.shape
    nc = rows // chunk
    blocks = wc // LANES
    steps = chunk // GROUP
    n_row = n_dp * n_mcol
    width = wc * n_row
    height = rows * n_mrow
    dp, mrow, mcol = lax.axis_index("dp"), lax.axis_index("mrow"), lax.axis_index("mcol")
    q = dp * n_mcol + mcol

    def dp_peer(k):
        return {"dp": lax.rem(dp + k, n_dp), "mrow": mrow, "mcol": mcol}

    def row_peer(k):
        other = lax.rem(q + k, n_row)
        return {"dp": other // n_mcol, "mrow": mrow, "mcol": lax.rem(other, n_mcol)}

    def col_peer(k):
        return {"dp": dp, "mrow": lax.rem(mrow + k, n_mrow), "mcol": mcol}

    def loop(lo, hi, body):
        lax.fori_loop(lo, hi, lambda i, c: (body(i), c)[1], 0)

    def part(i):
        return pl.ds(pl.multiple_of(i * chunk, chunk), chunk)

    def own_copy(i):
        cols = pl.ds(pl.multiple_of(dp * wc, LANES), wc)
        return pltpu.make_async_copy(grad_ref.at[0, part(i), cols], gbuf.at[part(i)], own_sem.at[i])

    def grad_copy(k, i):
        cols = pl.ds(pl.multiple_of(lax.rem(dp + k, n_dp) * wc, LANES), wc)
        return pltpu.make_async_remote_copy(
            src_ref=grad_ref.at[0, part(i), cols], dst_ref=recv.at[k - 1, part(i)],
            send_sem=gsend.at[k - 1, i], recv_sem=grecv.at[k - 1, i],
            device_id=dp_peer(k), device_id_type=MESH)

    def master_copy(i):
        return pltpu.make_async_copy(master_ref.at[part(i)], mbuf.at[part(i)], msem.at[i])

    def weight_copy(k, i):
        return pltpu.make_async_remote_copy(
            src_ref=recv.at[0, part(i)], dst_ref=w_recv_ref.at[n_dp - 1 - k, part(i)],
            send_sem=wsend.at[k - 1, i], recv_sem=wrecv.at[k - 1, i],
            device_id=dp_peer(k), device_id_type=MESH)

    def slot_copy(slots, index, peer, send, recv_, k):
        return pltpu.make_async_remote_copy(
            src_ref=slots.at[index], dst_ref=slots.at[index],
            send_sem=send.at[k], recv_sem=recv_.at[k],
            device_id=peer(k), device_id_type=MESH)

    def send_slots(slots, index, peer, send, recv_, n):
        loop(1, n, lambda k: slot_copy(slots, index, peer, send, recv_, k).start())

    def wait_slots(slots, index, peer, send, recv_, n):
        loop(1, n, lambda k: slot_copy(slots, index, peer, send, recv_, k).wait())

    loop(0, nc, lambda i: own_copy(i).start())

    barrier = pltpu.get_barrier_semaphore()
    loop(1, n_row, lambda k: pl.semaphore_signal(barrier, inc=1, device_id=row_peer(k), device_id_type=MESH))
    loop(1, n_mrow, lambda k: pl.semaphore_signal(barrier, inc=1, device_id=col_peer(k), device_id_type=MESH))
    pl.semaphore_wait(barrier, n_row + n_mrow - 2)

    loop(0, nc, lambda i: [grad_copy(k, i).start() for k in range(1, n_dp)])
    loop(0, nc, lambda i: master_copy(i).start())

    col_acc[...] = jnp.zeros_like(col_acc)

    def sum_chunk(i):
        own_copy(i).wait()
        for k in range(1, n_dp):
            grad_copy(k, i).wait_recv()
        base = i * chunk

        def sum_rows(s, carry):
            at = pl.ds(pl.multiple_of(base + s * GROUP, GROUP), GROUP)
            row = None
            for b in range(blocks):
                lanes = slice(b * LANES, (b + 1) * LANES)
                g = gbuf[at, lanes].astype(jnp.float32)
                for k in range(n_dp - 1):
                    g = g + recv[k, at, lanes].astype(jnp.float32)
                gbuf[at, lanes] = g.astype(jnp.bfloat16)
                square = g * g + SQUARE_FLOOR
                row = square if row is None else row + square
                col_acc[:, lanes] += square[:8] + square[8:]
            row_col[pl.ds(pl.multiple_of(base + s * GROUP, GROUP), GROUP), :] = row
            return carry

        lax.fori_loop(0, steps, sum_rows, 0)
        row_slots[q, :, part(i)] = jnp.sum(row_col[part(i), :].T, axis=0, keepdims=True)

    loop(0, nc, sum_chunk)
    col_slots[mrow] = jnp.sum(col_acc[...], axis=0, keepdims=True)
    send_slots(col_slots, mrow, col_peer, csend, crecv, n_mrow)
    send_slots(row_slots, q, row_peer, rsend, rrecv, n_row)
    wait_slots(row_slots, q, row_peer, rsend, rrecv, n_row)
    row_sum = row_slots[0]
    for j in range(1, n_row):
        row_sum = row_sum + row_slots[j]
    new_rows = DECAY_RATE * old_rows_ref[...] + (1.0 - DECAY_RATE) * row_sum / width
    new_rows_ref[...] = new_rows
    inv_rows[...] = lax.rsqrt(new_rows)
    row_mass = jnp.sum(new_rows)

    def spread(i):
        row_col[part(i), :] = jnp.broadcast_to(inv_rows[:, part(i)], (LANES, chunk)).T

    loop(0, nc, spread)
    wait_slots(col_slots, mrow, col_peer, csend, crecv, n_mrow)
    col_sum = lax.fori_loop(1, n_mrow, lambda j, acc: acc + col_slots[j], col_slots[0])
    new_cols = DECAY_RATE * old_cols_ref[...] + (1.0 - DECAY_RATE) * col_sum / height
    new_cols_ref[...] = new_cols
    inv_cols = 1.0 / new_cols
    col_acc[...] = jnp.broadcast_to(inv_cols, col_acc.shape)

    def square_rows(s, acc):
        at = pl.ds(pl.multiple_of(s * GROUP, GROUP), GROUP)
        row = None
        for b in range(blocks):
            lanes = slice(b * LANES, (b + 1) * LANES)
            g = gbuf[at, lanes].astype(jnp.float32)
            c = col_acc[:, lanes]
            term = g * g * jnp.concatenate([c, c], axis=0)
            row = term if row is None else row + term
        r = row_col[at, :]
        return acc + row * (r * r)

    acc = lax.fori_loop(0, rows // GROUP, square_rows, jnp.zeros((GROUP, LANES), jnp.float32))
    lane = lax.broadcasted_iota(jnp.int32, (1, LANES), 1)
    sc1_slots[mrow] = jnp.where(lane == 0, row_mass, jnp.where(lane == 1, jnp.sum(acc), 0.0))
    send_slots(sc1_slots, mrow, col_peer, s1send, s1recv, n_mrow)
    wait_slots(sc1_slots, mrow, col_peer, s1send, s1recv, n_mrow)
    sc2_slots[q] = lax.fori_loop(1, n_mrow, lambda j, a: a + sc1_slots[j], sc1_slots[0])
    send_slots(sc2_slots, q, row_peer, s2send, s2recv, n_row)
    wait_slots(sc2_slots, q, row_peer, s2send, s2recv, n_row)
    both = sc2_slots[0]
    for j in range(1, n_row):
        both = both + sc2_slots[j]
    total = jnp.sum(jnp.where(lane == 0, both, 0.0), axis=1, keepdims=True) / (n_row * height)
    whole = jnp.sum(jnp.where(lane == 1, both, 0.0), axis=1, keepdims=True)
    root_mean = jnp.sqrt(total * whole / (float(width) * float(height)))
    scale = jnp.sqrt(total) / jnp.maximum(1.0, root_mean / CLIP_LIMIT)
    scal_ref[0:1, :] = jnp.broadcast_to(root_mean, (1, LANES))
    scal_ref[1:2, :] = jnp.broadcast_to(scale, (1, LANES))
    col_acc[...] = jnp.broadcast_to(lax.rsqrt(new_cols) * scale, col_acc.shape)

    def weight_chunk(i):
        master_copy(i).wait()

        for k in range(1, n_dp):
            grad_copy(k, i).wait_send()

        def weight_rows(s, carry):
            at = pl.ds(pl.multiple_of(i * chunk + s * GROUP, GROUP), GROUP)
            r = row_col[at, :]
            for b in range(blocks):
                lanes = slice(b * LANES, (b + 1) * LANES)
                c = col_acc[:, lanes]
                step = gbuf[at, lanes].astype(jnp.float32) * r * jnp.concatenate([c, c], axis=0)
                new = mbuf[at, lanes] - LEARN_RATE * step
                mbuf[at, lanes] = new
                recv[0, at, lanes] = new.astype(jnp.bfloat16)
            return carry

        lax.fori_loop(0, steps, weight_rows, 0)
        for k in range(1, n_dp):
            weight_copy(k, i).start()

    loop(0, nc, weight_chunk)

    def finish(i):
        for k in range(1, n_dp):
            weight_copy(k, i).wait()

    loop(0, nc, finish)


def final_kernel(
    n_dp, chunk,
    g_ref, own_ref, w_recv_ref, master_ref, row_col, rows_ref, cols_ref, scal_ref,
    new_ref, weights_ref, step_ref, new_rows_ref, new_cols_ref, root_ref,
    sbuf, col_acc, nsem, wsem, rsem, ssem,
):
    rows, wc = g_ref.shape
    nc = rows // chunk
    slots = sbuf.shape[0]
    dp = lax.axis_index("dp")

    def loop(lo, hi, body):
        lax.fori_loop(lo, hi, lambda i, c: (body(i), c)[1], 0)

    def part(i):
        return pl.ds(pl.multiple_of(i * chunk, chunk), chunk)

    def cols_of(k):
        return pl.ds(pl.multiple_of(lax.rem(dp + k, n_dp) * wc, LANES), wc)

    def new_copy(i):
        return pltpu.make_async_copy(master_ref.at[part(i)], new_ref.at[part(i)], nsem.at[i])

    def own_copy(i):
        return pltpu.make_async_copy(own_ref.at[0, part(i)], weights_ref.at[part(i), cols_of(0)], wsem.at[i])

    def other_copy(k, i):
        return pltpu.make_async_copy(
            w_recv_ref.at[k - 1, part(i)], weights_ref.at[part(i), cols_of(k)], rsem.at[k - 1, i])

    def step_copy(i):
        slot = lax.rem(i, slots)
        return pltpu.make_async_copy(sbuf.at[slot], step_ref.at[part(i)], ssem.at[slot])

    def each(act):
        def body(i):
            act(new_copy(i))
            act(own_copy(i))
            for k in range(1, n_dp):
                act(other_copy(k, i))
        return body

    loop(0, nc, each(lambda copy: copy.start()))
    new_rows_ref[...] = rows_ref[...]
    new_cols_ref[...] = cols_ref[...]
    root_ref[0, 0] = jnp.max(scal_ref[0:1, :])
    col_acc[...] = jnp.broadcast_to(lax.rsqrt(cols_ref[...]) * scal_ref[1:2, 0:1], col_acc.shape)

    def step_chunk(i):
        slot = lax.rem(i, slots)

        @pl.when(i >= slots)
        def _():
            step_copy(i).wait()

        def body(s, carry):
            at = pl.ds(pl.multiple_of(s * GROUP, GROUP), GROUP)
            source = pl.ds(pl.multiple_of(i * chunk + s * GROUP, GROUP), GROUP)
            r = row_col[source, :]
            for b in range(wc // LANES):
                lanes = slice(b * LANES, (b + 1) * LANES)
                c = col_acc[:, lanes]
                sbuf[slot, at, lanes] = (
                    g_ref[source, lanes].astype(jnp.float32) * r * jnp.concatenate([c, c], axis=0))
            return carry

        lax.fori_loop(0, chunk // GROUP, body, 0)
        step_copy(i).start()

    loop(0, nc, step_chunk)
    loop(0, nc, each(lambda copy: copy.wait()))
    loop(max(nc - slots, 0), nc, lambda i: step_copy(i).wait())


def on_device(n_dp, n_mrow, n_mcol, grad_parts, master, row_factor, col_factor):
    rows, wc = master.shape
    chunk = chunk_of(rows)
    nc = rows // chunk
    n_row = n_dp * n_mcol
    f32, bf16 = jnp.float32, jnp.bfloat16
    dma = pltpu.SemaphoreType.DMA
    anywhere = pl.BlockSpec(memory_space=pl.ANY)
    vmem = pl.BlockSpec(memory_space=pltpu.VMEM)
    peers = max(n_dp - 1, 1)
    slots = min(3, nc)
    held = pl.pallas_call(
        functools.partial(stats_kernel, n_dp, n_mrow, n_mcol, chunk),
        out_shape=(
            pltpu.VMEM((rows, wc), bf16),
            pltpu.VMEM((peers, rows, wc), bf16),
            pltpu.VMEM((peers, rows, wc), bf16),
            pltpu.VMEM((rows, wc), f32),
            pltpu.VMEM((rows, LANES), f32),
            pltpu.VMEM((1, rows), f32),
            pltpu.VMEM((1, wc), f32),
            pltpu.VMEM((8, LANES), f32),
        ),
        in_specs=[anywhere, anywhere, vmem, vmem],
        out_specs=(vmem,) * 8,
        scratch_shapes=[
            pltpu.VMEM((n_row, 1, rows), f32),
            pltpu.VMEM((n_mrow, 1, wc), f32),
            pltpu.VMEM((n_mrow, 1, LANES), f32),
            pltpu.VMEM((n_row, 1, LANES), f32),
            pltpu.VMEM((1, rows), f32),
            pltpu.VMEM((8, wc), f32),
            dma((nc,)), dma((peers, nc)), dma((peers, nc)),
            dma((n_row,)), dma((n_row,)), dma((n_mrow,)), dma((n_mrow,)),
            dma((n_mrow,)), dma((n_mrow,)), dma((n_row,)), dma((n_row,)),
            dma((peers, nc)), dma((peers, nc)), dma((nc,)),
        ],
        compiler_params=pltpu.CompilerParams(
            collective_id=0, has_side_effects=True, vmem_limit_bytes=9 * 2**20
        ),
        name="stats",
    )(grad_parts, master, row_factor.reshape(1, rows), col_factor.reshape(1, wc))
    held = [pltpu.with_memory_space_constraint(x, pltpu.VMEM) for x in held]
    new_master, weights, step, new_rows, new_cols, root = pl.pallas_call(
        functools.partial(final_kernel, n_dp, chunk),
        out_shape=(
            jax.ShapeDtypeStruct((rows, wc), f32),
            jax.ShapeDtypeStruct((rows, n_dp * wc), bf16),
            jax.ShapeDtypeStruct((rows, wc), f32),
            jax.ShapeDtypeStruct((1, rows), f32),
            jax.ShapeDtypeStruct((1, wc), f32),
            jax.ShapeDtypeStruct((1, 1), f32),
        ),
        in_specs=[vmem] * 8,
        out_specs=(anywhere, anywhere, anywhere, vmem, vmem, pl.BlockSpec(memory_space=pltpu.SMEM)),
        scratch_shapes=[
            pltpu.VMEM((slots, chunk, wc), f32), pltpu.VMEM((8, wc), f32),
            dma((nc,)), dma((nc,)), dma((peers, nc)), dma((slots,)),
        ],
        compiler_params=pltpu.CompilerParams(vmem_limit_bytes=9 * 2**20),
        name="final",
    )(*held)
    return (
        new_master,
        weights,
        new_rows.reshape(rows),
        new_cols.reshape(wc),
        step,
        root.reshape(()),
    )


def solution(mesh):
    placed = (P("dp", "mrow", "mcol"), P("mrow", ("mcol", "dp")), P("mrow"), P(("mcol", "dp")))
    sizes = (mesh.shape["dp"], mesh.shape["mrow"], mesh.shape["mcol"])
    return jax.shard_map(
        functools.partial(on_device, *sizes),
        mesh=mesh,
        in_specs=placed,
        out_specs=(
            P("mrow", ("mcol", "dp")),
            P("mrow", "mcol"),
            P("mrow"),
            P(("mcol", "dp")),
            P("mrow", ("mcol", "dp")),
            P(),
        ),
        check_vma=False,
    )
```
